128 devices in a mesh: section: 4 (over y), seq: 16 (over x, z_hi, core), dp: 2 (over z_lo).
Axes of the slice: x: 4, y: 4, z: 4 (z_hi: 2, z_lo: 2; z = z_hi * 2 + z_lo), core: 2. Of those that a mesh axis runs over, the one named last changes fastest.
Arguments:
- roles: int32 [4], replicated, may hold values from 0 to 3, each once
- block_ids: int32 [2, 2, 3072], P(None, 'dp'), may hold values from 0 to 31, never falling along the last dimension, each value on 1 to 384 neighbouring positions
- latent: bfloat16 [2, 3072, 2560], P('dp', 'seq'), may hold values from -6 to 6
- pending: bfloat16 [2, 3072, 2560], P('dp', 'seq'), may hold values from -6 to 6
- context: float32 [2, 2560], P('dp'), may hold values from -6 to 6
- w_qkv: bfloat16 [3, 2560, 6144], P(None, None, 'seq'), may hold values from -3.3796842 to 3.3796842
- w_out: bfloat16 [3, 2048, 2560], P(None, 'seq'), may hold values from -0.125 to 0.125
- stored_attn: bfloat16 [2, 3072, 2048], P('dp', None, 'seq'), may hold values from -1.5 to 1.5
Outputs:
- block_out: bfloat16 [4, 2, 3072, 2560], P('section', 'dp', 'seq')
- dmd_grad: float32 [2, 3072, 2560], P('dp', 'seq')
- grad_out: float32 [2048, 2560], P('seq')
The draws below stay inside these ranges and needn't reach their ends.
Inputs may be any that keep to these rules, and one draw needn't show every extreme that they name: `roles`: each section has a different role: 0 generator, 1 teacher with context, 2 teacher without context, 3 fake-score model. `block_ids`: never falling along frames, starting at 0; each block has 1 to 384 frames, and one block of each row has exactly 384.
All inputs are finite; a program needn't handle non-finite values.
Results may differ from the reference program's by a relative error of at most 0.0083.
Values may be sent and summed in bfloat16 or wider, within the bound.
No kernel may reach another device: no remote copies, remote signals or barrier semaphores. Data moves between devices by JAX's collectives and lax.ppermute only.
A program may use at most 128 MiB of HBM per device.

```python
import math
import jax
import jax.numpy as jnp
import numpy as np
from jax import lax

D = 2560
HEADS = 16
HEAD_DIM = 128
MODELS = 3
L = 3072
INNER = 2048
SPANS = 32
SPAN_MOST = 384
N_SECTION = 4
N_DP = 2


def draw_w_qkv(key, part):
    base = jax.random.normal(key, (MODELS, D, HEADS, 3, HEAD_DIM), jnp.float32)
    factors = jnp.array([2.0 ** 0.5, 2.0 ** 0.5, 1.0], jnp.float32)
    weights = jnp.clip(base, -5.0, 5.0) * D ** (-0.5) * factors[None, None, None, :, None]
    return weights.reshape(MODELS, D, 3 * HEADS * HEAD_DIM).astype(jnp.bfloat16)


def level_of(rng, shape, pieces, least, largest):
    def one(dim, shards_of):
        steps = jax.random.uniform(jax.random.fold_in(jax.random.fold_in(rng, 6), dim), (shards_of,), jnp.float32, least / len(pieces), largest / len(pieces))
        return jnp.repeat(jnp.exp(steps), shape[dim] // shards_of).reshape((-1,) + (1,) * (len(shape) - dim - 1))

    loudness = one(*pieces[0])
    for cut in pieces[1:]:
        loudness = loudness * one(*cut)
    return loudness


def split_up(number_of, total, most, slope):
    weights = [(1 << 20) // math.isqrt(standing ** slope) + 1 for standing in range(2, number_of + 1)]
    spare, counts = total - most - (number_of - 1), [1] * (number_of - 1)
    while spare > 0:
        free = [i for i in range(number_of - 1) if counts[i] < most]
        pool, left = sum([weights[i] for i in free]), spare
        for i in free:
            addition = min(most - counts[i], max(1, left * weights[i] // pool), spare)
            counts[i] = counts[i] + addition
            spare = spare - addition
    return np.array([most] + counts)


def uneven_parts(key, amount, total, most, lean):
    if amount == 2:
        one = jax.random.randint(key, (), max(1, total - most), min(most, total - 1) + 1)
        return jnp.stack([one, total - one])
    lengths = jnp.asarray(split_up(amount, total, most, lean), jnp.int32)
    couples = (amount - 1) // 2
    giver, taker = lengths[1:1 + 2 * couples:2], lengths[2:2 + 2 * couples:2]
    margin = jnp.minimum(giver - 1, most - taker)
    passed = jax.random.randint(jax.random.fold_in(key, 1), (couples,), 0, 1 << 20) % (margin + 1)
    lengths = lengths.at[1:1 + 2 * couples:2].set(giver - passed).at[2:2 + 2 * couples:2].set(taker + passed)
    return lengths[jax.random.permutation(jax.random.fold_in(key, 2), amount)]


def gaussian(rng, extent, width, bound, cuts=(), held_as=jnp.bfloat16):
    gain = level_of(rng, extent, cuts, -0.22, 0.18) if cuts else 1.0
    values = jax.random.normal(rng, extent, jnp.float32) * width * gain
    return jnp.minimum(jnp.maximum(values, -bound), bound).astype(held_as)


def setup_inputs(seed: int = 0) -> dict:
    key_list = jax.random.split(jax.random.key(seed), 9)
    roles = jax.random.permutation(key_list[0], 4).astype(jnp.int32)
    block_ids = jax.vmap(lambda own: jnp.searchsorted(jnp.cumsum(uneven_parts(own, SPANS, L, SPAN_MOST, 2)), jnp.arange(L), side="right"))(jax.random.split(key_list[1], 2 * N_DP)).reshape((2, N_DP, L)).astype(jnp.int32)
    latent = gaussian(key_list[2], (N_DP, L, D), 1.0, 6.0, ((0, 2), (1, 16)))
    pending = gaussian(key_list[3], (N_DP, L, D), 1.0, 6.0, ((0, 2), (1, 16)))
    context = gaussian(key_list[4], (N_DP, D), 1.0, 6.0, ((0, 2),), jnp.float32)
    w_qkv = draw_w_qkv(jax.random.fold_in(key_list[8], 71), 0)
    w_out = gaussian(key_list[6], (MODELS, INNER, D), INNER ** -0.5, 0.125, ((1, 16),))
    stored_attn = gaussian(key_list[7], (N_DP, L, INNER), 0.25, 1.5, ((0, 2), (2, 16)))
    return dict(roles=roles, block_ids=block_ids, latent=latent, pending=pending, context=context, w_qkv=w_qkv, w_out=w_out, stored_attn=stored_attn)


GUIDE = 3.0
EPSILON = 1e-06
NEGATIVE = -1e+30

def attend(qkv_rows, frame_ids):
    length = qkv_rows.shape[0]
    split = qkv_rows.reshape(length, HEADS, 3, HEAD_DIM).transpose(1, 2, 0, 3)
    block_size = min(512, length)
    block_count = length // block_size
    scale = HEAD_DIM ** (-0.5)

    def per_head(triple):
        queries = triple[0]
        keys_all = triple[1]
        values = triple[2]

        def per_block(args):
            query_rows, query_ids = args
            scores = lax.dot_general(query_rows, keys_all, (((1,), (1,)), ((), ())), preferred_element_type=jnp.float32) * scale
            visible = frame_ids[None, :] <= query_ids[:, None]
            scores = jnp.where(visible, scores, NEGATIVE)
            highest = lax.optimization_barrier(jnp.max(scores, axis=1, keepdims=True))
            expon = jnp.where(visible, jnp.exp(scores - highest), 0.0)
            probs = (expon / lax.optimization_barrier(jnp.sum(expon, axis=1, keepdims=True))).astype(jnp.bfloat16)
            return jnp.dot(probs, values, preferred_element_type=jnp.float32).astype(jnp.bfloat16)
        blocks = lax.map(per_block, (queries.reshape(block_count, block_size, HEAD_DIM), frame_ids.reshape(block_count, block_size)))
        return blocks.reshape(length, HEAD_DIM)
    heads_out = lax.map(per_head, split)
    return heads_out.transpose(1, 0, 2).reshape(length, HEADS * HEAD_DIM)

def reference(roles, block_ids, latent, pending, context, w_qkv, w_out, stored_attn):
    places = jnp.arange(4, dtype=jnp.int32)
    model_table = jnp.array([0, 1, 1, 2], jnp.int32)
    weight_table = jnp.array([0.0, -GUIDE, GUIDE - 1.0, 1.0], jnp.float32)
    section_outs = []
    gradient = jnp.zeros((N_DP, L, D), jnp.float32)
    for place in range(N_SECTION):
        section_role = roles[place]
        model_index = jnp.sum(jnp.where(places == section_role, model_table, 0)).astype(jnp.int32)
        score_weight = jnp.sum(jnp.where(places == section_role, weight_table, 0.0))
        w_in = lax.dynamic_index_in_dim(w_qkv, model_index, 0, keepdims=False)
        w_proj = lax.dynamic_index_in_dim(w_out, model_index, 0, keepdims=False)
        is_generator = section_role == 0
        with_context = jnp.logical_or(section_role == 1, section_role == 3).astype(jnp.float32)
        sequence_outs = []
        for seq_index in range(N_DP):
            scored = pending[seq_index].astype(jnp.float32) + with_context * context[seq_index][None, :]
            source = jnp.where(is_generator, latent[seq_index].astype(jnp.float32), scored)
            normed = (source * lax.rsqrt(lax.optimization_barrier(jnp.mean(source * source, axis=1, keepdims=True)) + EPSILON)).astype(jnp.bfloat16)
            qkv_rows = jnp.dot(normed, w_in, preferred_element_type=jnp.float32).astype(jnp.bfloat16)
            frame_ids = jnp.where(is_generator, block_ids[0, seq_index], block_ids[1, seq_index])
            attn = attend(qkv_rows, frame_ids)
            branch = jnp.dot(attn, w_proj, preferred_element_type=jnp.float32)
            sequence_outs.append((source + branch).astype(jnp.bfloat16))
            gradient = gradient.at[seq_index].add(score_weight * branch)
        section_outs.append(jnp.stack(sequence_outs))
    block_out = jnp.stack(section_outs)
    grad_bf = gradient.astype(jnp.bfloat16)
    grad_out = jnp.zeros((INNER, D), jnp.float32)
    for seq_index in range(N_DP):
        grad_out = grad_out + jnp.dot(stored_attn[seq_index].T, grad_bf[seq_index], preferred_element_type=jnp.float32)
    return (block_out, gradient, grad_out)
```

```python
import jax
import jax.numpy as jnp
import numpy as np
from jax import lax
from jax.experimental import pallas as pl
from jax.experimental.pallas import tpu as pltpu
from jax.sharding import Mesh
from jax.sharding import PartitionSpec as P

HEAD_DIM = 128
GUIDE = 3.0
EPSILON = 1e-06
NEGATIVE = -1e30
QUERY_TILE = 512
KEY_TILE = 512
LOG2E = 1.4426950408889634
RING = ("x", "zhi")
SEQ = ("x", "zhi", "core")


def attention_kernel(bounds, qkv, seen, out, values, top, acc):
    tile = pl.program_id(0)
    length = qkv.shape[0]

    @pl.when(tile == 0)
    def _():
        values[:, :HEAD_DIM] = qkv[:, 2 * HEAD_DIM :]
        values[:, HEAD_DIM:] = jnp.ones((length, HEAD_DIM), jnp.bfloat16)

    start = pl.multiple_of(tile * QUERY_TILE, QUERY_TILE)
    queries = qkv[pl.ds(start, QUERY_TILE), :HEAD_DIM]
    factor = LOG2E * HEAD_DIM ** (-0.5)
    top[...] = jnp.full(top.shape, NEGATIVE, jnp.float32)
    acc[...] = jnp.zeros(acc.shape, jnp.float32)

    def step(j, masked):
        first = pl.multiple_of(j * KEY_TILE, KEY_TILE)
        keys = qkv[pl.ds(first, KEY_TILE), HEAD_DIM : 2 * HEAD_DIM]
        scores = lax.dot_general(
            queries, keys, (((1,), (1,)), ((), ())), preferred_element_type=jnp.float32
        ) * factor
        if masked:
            place = lax.broadcasted_iota(jnp.int32, scores.shape, 1) + first
            scores = jnp.where(place < seen[...], scores, NEGATIVE)
        old = top[...]
        new = jnp.maximum(old, jnp.max(scores, axis=1, keepdims=True))
        top[...] = new
        weights = jnp.exp2(scores - new).astype(jnp.bfloat16)
        acc[...] = acc[...] * jnp.exp2(old - new) + jnp.dot(
            weights, values[pl.ds(first, KEY_TILE), :], preferred_element_type=jnp.float32
        )

    whole = bounds[tile, 0]

    @pl.loop(0, whole)
    def _(j):
        step(j, False)

    @pl.loop(whole, bounds[tile, 1])
    def _(j):
        step(j, True)

    out[...] = (acc[:, :HEAD_DIM] / acc[:, HEAD_DIM:]).astype(jnp.bfloat16)


def attend(qkv_rows, frame_ids):
    length = qkv_rows.shape[0]
    tiles = length // QUERY_TILE
    seen = jnp.sum((frame_ids[None, :] <= frame_ids[:, None]).astype(jnp.int32), axis=1)
    per_tile = seen.reshape(tiles, QUERY_TILE)
    bounds = jnp.stack(
        [per_tile[:, 0] // KEY_TILE, (per_tile[:, -1] + KEY_TILE - 1) // KEY_TILE], axis=1
    )
    return pl.pallas_call(
        attention_kernel,
        out_shape=jax.ShapeDtypeStruct((length, HEAD_DIM), jnp.bfloat16),
        grid_spec=pltpu.PrefetchScalarGridSpec(
            num_scalar_prefetch=1,
            grid=(tiles,),
            in_specs=[
                pl.BlockSpec((length, 3 * HEAD_DIM), lambda i, b: (0, 0)),
                pl.BlockSpec((QUERY_TILE, 1), lambda i, b: (i, 0)),
            ],
            out_specs=pl.BlockSpec((QUERY_TILE, HEAD_DIM), lambda i, b: (i, 0)),
            scratch_shapes=[
                pltpu.VMEM((length, 2 * HEAD_DIM), jnp.bfloat16),
                pltpu.VMEM((QUERY_TILE, 1), jnp.float32),
                pltpu.VMEM((QUERY_TILE, 2 * HEAD_DIM), jnp.float32),
            ],
        ),
        name="attend",
    )(bounds, qkv_rows, seen[:, None])


def per_device(roles, block_ids, latent, pending, context, w_qkv, w_out, stored_attn):
    section = lax.axis_index("section")
    places = jnp.arange(4, dtype=jnp.int32)
    weight_table = jnp.array([0.0, -GUIDE, GUIDE - 1.0, 1.0], jnp.float32)
    section_role = jnp.sum(jnp.where(places == section, roles, 0))
    model_index = jnp.sum(jnp.where(places == section_role, jnp.array([0, 1, 1, 2], jnp.int32), 0))
    own_weight = jnp.sum(jnp.where(places == section_role, weight_table, 0.0))
    w_in = lax.dynamic_index_in_dim(w_qkv, model_index, 0, keepdims=False)
    w_proj = lax.dynamic_index_in_dim(w_out, model_index, 0, keepdims=False)
    is_generator = section_role == 0
    with_context = jnp.logical_or(section_role == 1, section_role == 3).astype(jnp.float32)
    rows, width = latent.shape[1:]
    scored = pending[0].astype(jnp.float32) + with_context * context[0][None, :]
    source = jnp.where(is_generator, latent[0].astype(jnp.float32), scored)
    normed = (
        source * lax.rsqrt(jnp.mean(source * source, axis=1, keepdims=True) + EPSILON)
    ).astype(jnp.bfloat16)
    qkv_rows = jnp.dot(
        lax.all_gather(normed, SEQ, axis=0, tiled=True), w_in, preferred_element_type=jnp.float32
    ).astype(jnp.bfloat16)
    frame_ids = jnp.where(is_generator, block_ids[0, 0], block_ids[1, 0])
    attn = attend(qkv_rows, frame_ids)
    local_attn = lax.all_to_all(attn, SEQ, split_axis=0, concat_axis=1, tiled=True)
    branch = jnp.dot(
        local_attn,
        lax.all_gather(w_proj, SEQ, axis=0, tiled=True),
        preferred_element_type=jnp.float32,
    )
    block_out = (source + branch).astype(jnp.bfloat16)[None, None]
    return (block_out,) + gradients(own_weight, branch, stored_attn)


def gradients(own_weight, branch, stored_attn):
    rows, width = branch.shape
    sections = lax.axis_size("section")
    part = width // sections
    terms = (own_weight * branch).astype(jnp.bfloat16)
    terms = terms.reshape(rows, sections, part).transpose(1, 0, 2)
    terms = lax.all_to_all(terms, "section", 0, 0, tiled=True)
    grad_bf = jnp.sum(terms.astype(jnp.float32), axis=0).astype(jnp.bfloat16)
    gradient = lax.all_gather(grad_bf, "section", axis=1, tiled=True).astype(jnp.float32)[None]
    core = lax.axis_index("core")
    other = lax.ppermute(grad_bf, "core", [(0, 1), (1, 0)])
    both = jnp.where(core == 0, jnp.stack([grad_bf, other]), jnp.stack([other, grad_bf]))
    both = both.reshape(2 * rows, part)
    chips = lax.axis_size("x") * lax.axis_size("zhi")
    inner_here = stored_attn.shape[2]
    stored = lax.all_to_all(
        stored_attn.reshape(chips, 2 * rows, inner_here), RING, 0, 0, tiled=True
    )
    product = jnp.einsum("hri,rc->hic", stored, both, preferred_element_type=jnp.float32)
    product = product.astype(jnp.bfloat16).reshape(chips, inner_here, 2, part // 2)
    product = product.transpose(0, 2, 1, 3).reshape(chips * 2, inner_here, part // 2)
    product = lax.all_to_all(product, RING + ("dp",), 0, 0, tiled=True)
    total = jnp.sum(product.astype(jnp.float32), axis=0).astype(jnp.bfloat16)
    grad_out = lax.all_gather(total, ("section", "dp"), axis=1, tiled=True).astype(jnp.float32)
    return (gradient, grad_out)


def solution(mesh):
    fine = Mesh(mesh.devices.reshape(4, 4, 2, 2, 2), ("section", "x", "zhi", "core", "dp"))
    placed = (
        P(),
        P(None, "dp", None),
        P("dp", SEQ, None),
        P("dp", SEQ, None),
        P("dp", None),
        P(None, None, SEQ),
        P(None, SEQ, None),
        P("dp", None, SEQ),
    )
    return jax.shard_map(
        per_device,
        mesh=fine,
        in_specs=placed,
        out_specs=(P("section", "dp", SEQ, None), P("dp", SEQ, None), P(SEQ, None)),
        check_vma=False,
    )
```

```python
import jax
import jax.numpy as jnp
from jax import lax
from jax.experimental import pallas as pl
from jax.experimental.pallas import tpu as pltpu
from jax.sharding import Mesh
from jax.sharding import PartitionSpec as P


HEAD_DIM = 128
GUIDE = 3.0
EPSILON = 1e-06
NEGATIVE = -1e30
QUERY_TILE = 512
QUERY_PART = 256
KEY_TILE = 512
SCORE_SCALE = 1.4426950408889634 * HEAD_DIM ** (-0.5)
RING = ("x", "zhi")
SEQ = ("x", "zhi", "core")
SWAP = [(0, 1), (1, 0)]


def attention_kernel(bounds, starts, *refs):
    pieces = refs[:8]
    seen, out, qkv, values, top, acc, sems = refs[8:]
    tile = pl.program_id(0)
    length = qkv.shape[0]
    chips = 8
    chunk = pieces[0].shape[0] // chips

    @pl.when(tile == 0)
    def _():
        copies = []
        for i, piece in enumerate(pieces):
            for b in range(chips):
                place = pl.multiple_of(starts[i] * chunk + b * (length // chips), chunk)
                copies.append(
                    pltpu.make_async_copy(
                        piece.at[pl.ds(b * chunk, chunk)],
                        qkv.at[pl.ds(place, chunk)],
                        sems.at[i, b],
                    )
                )
        for copy in copies:
            copy.start()
        for copy in copies:
            copy.wait()
        values[:, :HEAD_DIM] = qkv[:, 2 * HEAD_DIM :]
        values[:, HEAD_DIM:] = jnp.ones((length, HEAD_DIM), jnp.bfloat16)

    top[...] = jnp.full(top.shape, NEGATIVE, jnp.float32)
    acc[...] = jnp.zeros(acc.shape, jnp.float32)
    parts = QUERY_TILE // QUERY_PART

    def step(j, masked):
        first = pl.multiple_of(j * KEY_TILE, KEY_TILE)
        keys = qkv[pl.ds(first, KEY_TILE), HEAD_DIM : 2 * HEAD_DIM]
        value = values[pl.ds(first, KEY_TILE), :]
        scores = []
        for i in range(parts):
            start = pl.multiple_of(tile * QUERY_TILE + i * QUERY_PART, QUERY_PART)
            score = lax.dot_general(
                qkv[pl.ds(start, QUERY_PART), :HEAD_DIM],
                keys,
                (((1,), (1,)), ((), ())),
                preferred_element_type=jnp.float32,
            )
            if masked:
                place = lax.broadcasted_iota(jnp.int32, score.shape, 1) + first
                limit = seen[pl.ds(i * QUERY_PART, QUERY_PART), :]
                score = jnp.where(place < limit, score, NEGATIVE)
            scores.append(score)
        olds = [top[i] for i in range(parts)]
        news = [
            jnp.maximum(old, jnp.max(score, axis=1, keepdims=True))
            for old, score in zip(olds, scores)
        ]
        for i in range(parts):
            weights = jnp.exp2(scores[i] - news[i]).astype(jnp.bfloat16)
            acc[i] = acc[i] * jnp.exp2(olds[i] - news[i]) + jnp.dot(
                weights, value, preferred_element_type=jnp.float32
            )
            top[i] = news[i]

    whole = bounds[tile, 0]

    @pl.loop(0, whole)
    def _(j):
        step(j, False)

    @pl.loop(whole, bounds[tile, 1])
    def _(j):
        step(j, True)

    for i in range(parts):
        out[pl.ds(i * QUERY_PART, QUERY_PART), :] = (
            acc[i, :, :HEAD_DIM] / acc[i, :, HEAD_DIM:]
        ).astype(jnp.bfloat16)


def visibility(frame_ids):
    length = frame_ids.shape[0]
    tiles = length // QUERY_TILE
    seen = jnp.sum((frame_ids[None, :] <= frame_ids[:, None]).astype(jnp.int32), axis=1)
    per_tile = seen.reshape(tiles, QUERY_TILE)
    bounds = jnp.stack(
        [per_tile[:, 0] // KEY_TILE, (per_tile[:, -1] + KEY_TILE - 1) // KEY_TILE], axis=1
    )
    return seen[:, None], bounds


def attend(pieces, starts, seen, bounds):
    length = seen.shape[0]
    wide = pieces[0].shape[1]
    parts = QUERY_TILE // QUERY_PART
    return pl.pallas_call(
        attention_kernel,
        out_shape=jax.ShapeDtypeStruct((length, HEAD_DIM), jnp.bfloat16),
        grid_spec=pltpu.PrefetchScalarGridSpec(
            num_scalar_prefetch=2,
            grid=(length // QUERY_TILE,),
            in_specs=[pl.BlockSpec(memory_space=pl.ANY)] * 8
            + [pl.BlockSpec((QUERY_TILE, 1), lambda i, b, s: (i, 0))],
            out_specs=pl.BlockSpec((QUERY_TILE, HEAD_DIM), lambda i, b, s: (i, 0)),
            scratch_shapes=[
                pltpu.VMEM((length, wide), jnp.bfloat16),
                pltpu.VMEM((length, 2 * HEAD_DIM), jnp.bfloat16),
                pltpu.VMEM((parts, QUERY_PART, 1), jnp.float32),
                pltpu.VMEM((parts, QUERY_PART, 2 * HEAD_DIM), jnp.float32),
                pltpu.SemaphoreType.DMA((8, 8)),
            ],
        ),
        name="attend",
    )(bounds, starts, *pieces, seen)


def project_kernel(place, *refs):
    rows = refs[:10]
    context, w_mine, w_other = refs[10:13]
    outs, (sources, scales) = refs[13:21], refs[21:]
    step = pl.program_id(0)
    chunk = rows[0].shape[1]

    @pl.when(step == 0)
    def _():
        added = context[...]
        for side in range(2):
            own, right, far_scored, far_latent, left = rows[side * 5 : side * 5 + 5]
            found = [(own[0], own[1]), (right[0], right[1])]
            found += [(far_scored[...], far_latent[...]), (left[0], left[1])]
            for i, (scored, latent) in enumerate(found):
                at = pl.ds(pl.multiple_of(place[4 + side * 4 + i] * chunk, chunk), chunk)
                wide = scored.astype(jnp.float32)
                shifted = wide + added
                sources[0, at, :] = scored
                sources[1, at, :] = shifted.astype(jnp.bfloat16)
                sources[2, at, :] = latent
                for j, v in enumerate((wide, shifted, latent.astype(jnp.float32))):
                    scales[j, at, :] = lax.rsqrt(
                        jnp.mean(v * v, axis=1, keepdims=True) + EPSILON
                    )

    role = place[step]
    kind = jnp.where(role == 0, 2, role % 2)
    left = sources[kind]
    scale = scales[kind]
    made = [
        jnp.dot(left, weights[0], preferred_element_type=jnp.float32) * scale
        for weights in (w_mine, w_other)
    ]
    for i in range(4):

        @pl.when(step == i)
        def _():
            for side in range(2):
                out = outs[2 * i + side]
                out[:, :HEAD_DIM] = (made[side][:, :HEAD_DIM] * SCORE_SCALE).astype(jnp.bfloat16)
                out[:, HEAD_DIM:] = made[side][:, HEAD_DIM:].astype(jnp.bfloat16)


def project(place, rows, context, w_mine, w_other):
    chunk, width = rows[0].shape[1:]
    many = 8 * chunk
    columns = w_mine.shape[2]
    picked = pl.BlockSpec((1, width, columns), lambda t, r: ((r[t] + 1) // 2, 0, 0))
    whole = pl.BlockSpec(memory_space=pltpu.VMEM)
    return pl.pallas_call(
        project_kernel,
        out_shape=[jax.ShapeDtypeStruct((many, columns), jnp.bfloat16)] * 8,
        grid_spec=pltpu.PrefetchScalarGridSpec(
            num_scalar_prefetch=1,
            grid=(4,),
            in_specs=[whole] * 11 + [picked, picked],
            out_specs=[pl.BlockSpec((many, columns), lambda t, r: (0, 0))] * 8,
            scratch_shapes=[
                pltpu.VMEM((3, many, width), jnp.bfloat16),
                pltpu.VMEM((3, many, 1), jnp.float32),
            ],
        ),
        name="project",
    )(place, *rows, context, w_mine, w_other)


def place_kernel(starts, *refs):
    out = refs[-1]
    for i, piece in enumerate(refs[:-1]):
        rows, columns = piece.shape
        row = pl.multiple_of(starts[i, 0], rows)
        column = pl.multiple_of(starts[i, 1], columns)
        out[pl.ds(row, rows), pl.ds(column, columns)] = piece[...].astype(jnp.float32)


def place_all(starts, pieces, shape):
    vmem = pl.BlockSpec(memory_space=pltpu.VMEM)
    return pl.pallas_call(
        place_kernel,
        out_shape=jax.ShapeDtypeStruct(shape, jnp.float32),
        in_specs=[pl.BlockSpec(memory_space=pltpu.SMEM)] + [vmem] * len(pieces),
        out_specs=vmem,
        name="place_all",
    )(starts, *pieces)


def moved(axis, size, step):
    return [(i, (i + step) % size) for i in range(size)]


def moved(axis, size, step):
    return [(i, (i + step) % size) for i in range(size)]


def per_device(roles, block_ids, latent, pending, context, w_qkv, w_out, stored_attn):
    section, core = lax.axis_index("section"), lax.axis_index("core")
    section_role = lax.dynamic_index_in_dim(roles, section, 0, keepdims=False)
    own_weight = jnp.where(
        section_role == 1,
        -GUIDE,
        jnp.where(section_role == 2, GUIDE - 1.0, jnp.where(section_role == 3, 1.0, 0.0)),
    )
    is_generator = section_role == 0
    with_context = (section_role % 2).astype(jnp.float32)
    rows, _ = latent.shape[1:]
    chunk = rows // lax.axis_size("section")

    quarter = jnp.stack(
        [
            lax.dynamic_slice_in_dim(pending[0], section * chunk, chunk, 0),
            lax.dynamic_slice_in_dim(latent[0], section * chunk, chunk, 0),
        ]
    )
    w_proj = lax.dynamic_index_in_dim(w_out, (section_role + 1) // 2, 0, keepdims=False)
    inner = w_proj.shape[0]
    w_wide = jnp.broadcast_to(w_proj[None], (8,) + w_proj.shape)
    frame_ids = jnp.where(is_generator, block_ids[0, 0], block_ids[1, 0])
    seen, bounds = visibility(frame_ids)

    theirs = lax.ppermute(quarter, "zhi", SWAP)
    everything = []
    for ours in (quarter, theirs):
        left = lax.ppermute(ours, "x", moved("x", 4, 1))
        right = lax.ppermute(ours, "x", moved("x", 4, -1))
        far_scored = lax.ppermute(left[0], "x", moved("x", 4, 1))
        far_latent = lax.ppermute(right[1], "x", moved("x", 4, -1))
        everything += [ours, right, far_scored, far_latent, left]
    everything, w_wide = lax.optimization_barrier((everything, w_wide))
    w_other = lax.ppermute(w_qkv, "core", SWAP)
    ahead = jnp.arange(4, dtype=jnp.int32)
    near = (lax.axis_index("x") + ahead) % 4 * 2
    zhi = lax.axis_index("zhi")
    place = jnp.concatenate(
        [jnp.roll(roles, -section), near + zhi, near + (1 - zhi)]
    )
    made = project(place, everything, context, w_qkv, w_other)
    w_mine = lax.all_to_all(w_wide, RING, 0, 0, tiled=True)
    pieces = [made[0]]
    for i in range(1, 8):
        step, side = i // 2, i % 2
        perm = [
            (s * 2 + c, (s + step) % 4 * 2 + (c + side) % 2) for s in range(4) for c in range(2)
        ]
        pieces.append(lax.ppermute(made[i], ("section", "core"), perm))
    starts = jnp.arange(8, dtype=jnp.int32)
    starts = (core + starts) % 2 * 4 + (section - starts // 2) % 4
    attn = attend(pieces, starts, seen, bounds)
    attn, w_mine = lax.optimization_barrier((attn, w_mine))
    w_theirs = lax.ppermute(w_mine, "core", SWAP)
    attn = lax.all_to_all(attn.reshape(16, rows, inner), SEQ, 0, 0, tiled=True)
    attn, stored_attn = lax.optimization_barrier((attn, stored_attn))
    stored = lax.all_to_all(stored_attn.reshape(8, 2 * rows, inner), RING, 0, 0, tiled=True)
    attn = attn.reshape(8, 2, rows, inner)
    mine = lax.dynamic_index_in_dim(attn, core, 1, keepdims=False)
    theirs = lax.dynamic_index_in_dim(attn, 1 - core, 1, keepdims=False)
    branch = jnp.einsum(
        "hri,hic->rc", mine, w_mine, preferred_element_type=jnp.float32
    ) + jnp.einsum("hri,hic->rc", theirs, w_theirs, preferred_element_type=jnp.float32)
    held = pending[0].astype(jnp.float32) + with_context * context[0][None, :]
    source = jnp.where(is_generator, latent[0].astype(jnp.float32), held)
    block_out = (source + branch).astype(jnp.bfloat16)[None, None]
    return (block_out,) + gradients(own_weight, branch, stored)


def gradients(own_weight, branch, stored):
    rows, width = branch.shape
    sections = lax.axis_size("section")
    section, core = lax.axis_index("section"), lax.axis_index("core")
    part = width // sections
    terms = (own_weight * branch).astype(jnp.bfloat16)
    total = None
    for step in (2, 1, 3, 0):
        column = (section + step) % sections * part
        term = lax.dynamic_slice_in_dim(terms, column, part, 1)
        if step:
            term = lax.ppermute(term, "section", moved("section", sections, step))
        total = term.astype(jnp.float32) + (0.0 if total is None else total)
    grad_bf = total.astype(jnp.bfloat16)
    other = lax.ppermute(grad_bf, "core", SWAP)
    both = jnp.where(core == 0, jnp.stack([grad_bf, other]), jnp.stack([other, grad_bf]))
    both = both.reshape(2 * rows, part)
    inner = stored.shape[2]
    product = jnp.einsum("hri,rc->hic", stored, both, preferred_element_type=jnp.float32)
    product = product.astype(jnp.bfloat16).reshape(16, inner // 2, part)
    product = lax.all_to_all(product, RING + ("dp",), 0, 0, tiled=True)
    summed = jnp.sum(product.astype(jnp.float32), axis=0).astype(jnp.bfloat16)
    summed = jnp.broadcast_to(summed[None], (8,) + summed.shape)
    summed = lax.all_to_all(summed, ("section", "dp"), 0, 0, tiled=True)
    grad_out = summed.reshape(4, 2, inner // 2, part).transpose(1, 2, 0, 3)
    grad_out = grad_out.reshape(inner, width).astype(jnp.float32)
    groups, starts = [grad_bf], [section * part]
    for step in (2, 1, 3):
        groups.append(lax.ppermute(grad_bf, "section", moved("section", sections, step)))
        starts.append((section - step) % sections * part)
    gradient = place_all(
        jnp.stack([jnp.stack([jnp.zeros_like(s), s]) for s in starts]), groups, (rows, width)
    )
    return (gradient[None], grad_out)


def solution(mesh):
    fine = Mesh(mesh.devices.reshape(4, 4, 2, 2, 2), ("section", "x", "zhi", "core", "dp"))
    placed = (
        P(),
        P(None, "dp", None),
        P("dp", SEQ, None),
        P("dp", SEQ, None),
        P("dp", None),
        P(None, None, SEQ),
        P(None, SEQ, None),
        P("dp", None, SEQ),
    )
    return jax.shard_map(
        per_device,
        mesh=fine,
        in_specs=placed,
        out_specs=(P("section", "dp", SEQ, None), P("dp", SEQ, None), P(SEQ, None)),
        check_vma=False,
    )
```

```python
import jax
import jax.numpy as jnp
from jax import lax
from jax.experimental import pallas as pl
from jax.experimental.pallas import tpu as pltpu
from jax.sharding import Mesh
from jax.sharding import PartitionSpec as P


HEAD_DIM = 128
GUIDE = 3.0
EPSILON = 1e-06
NEGATIVE = -1e30
QUERY_TILE = 512
QUERY_PART = 256
KEY_TILE = 512
SCORE_SCALE = 1.4426950408889634 * HEAD_DIM ** (-0.5)
RING = ("x", "zhi")
SEQ = ("x", "zhi", "core")
SWAP = [(0, 1), (1, 0)]


def attention_kernel(bounds, starts, *refs):
    pieces = refs[:16]
    seen, out, qkv, values, top, acc, sems = refs[16:]
    tile = pl.program_id(0)
    length = qkv.shape[0]
    ring = 4
    chunk = pieces[0].shape[0] // ring

    @pl.when(tile == 0)
    def _():
        copies = []
        for i, piece in enumerate(pieces):
            for b in range(ring):
                place = pl.multiple_of(starts[i] * chunk + b * (length // ring), chunk)
                copies.append(
                    pltpu.make_async_copy(
                        piece.at[pl.ds(b * chunk, chunk)],
                        qkv.at[pl.ds(place, chunk)],
                        sems.at[i, b],
                    )
                )
        for copy in copies:
            copy.start()
        for copy in copies:
            copy.wait()
        values[:, :HEAD_DIM] = qkv[:, 2 * HEAD_DIM :]
        values[:, HEAD_DIM:] = jnp.ones((length, HEAD_DIM), jnp.bfloat16)

    top[...] = jnp.full(top.shape, NEGATIVE, jnp.float32)
    acc[...] = jnp.zeros(acc.shape, jnp.float32)
    parts = QUERY_TILE // QUERY_PART

    def step(j, masked):
        first = pl.multiple_of(j * KEY_TILE, KEY_TILE)
        keys = qkv[pl.ds(first, KEY_TILE), HEAD_DIM : 2 * HEAD_DIM]
        value = values[pl.ds(first, KEY_TILE), :]
        scores = []
        for i in range(parts):
            start = pl.multiple_of(tile * QUERY_TILE + i * QUERY_PART, QUERY_PART)
            score = lax.dot_general(
                qkv[pl.ds(start, QUERY_PART), :HEAD_DIM],
                keys,
                (((1,), (1,)), ((), ())),
                preferred_element_type=jnp.float32,
            )
            if masked:
                place = lax.broadcasted_iota(jnp.int32, score.shape, 1) + first
                limit = seen[pl.ds(i * QUERY_PART, QUERY_PART), :]
                score = jnp.where(place < limit, score, NEGATIVE)
            scores.append(score)
        olds = [top[i] for i in range(parts)]
        news = [
            jnp.maximum(old, jnp.max(score, axis=1, keepdims=True))
            for old, score in zip(olds, scores)
        ]
        for i in range(parts):
            weights = jnp.exp2(scores[i] - news[i]).astype(jnp.bfloat16)
            acc[i] = acc[i] * jnp.exp2(olds[i] - news[i]) + jnp.dot(
                weights, value, preferred_element_type=jnp.float32
            )
            top[i] = news[i]

    whole = bounds[tile, 0]

    @pl.loop(0, whole)
    def _(j):
        step(j, False)

    @pl.loop(whole, bounds[tile, 1])
    def _(j):
        step(j, True)

    for i in range(parts):
        out[pl.ds(i * QUERY_PART, QUERY_PART), :] = (
            acc[i, :, :HEAD_DIM] / acc[i, :, HEAD_DIM:]
        ).astype(jnp.bfloat16)


def visibility(frame_ids):
    length = frame_ids.shape[0]
    tiles = length // QUERY_TILE
    seen = jnp.sum((frame_ids[None, :] <= frame_ids[:, None]).astype(jnp.int32), axis=1)
    per_tile = seen.reshape(tiles, QUERY_TILE)
    bounds = jnp.stack(
        [per_tile[:, 0] // KEY_TILE, (per_tile[:, -1] + KEY_TILE - 1) // KEY_TILE], axis=1
    )
    return seen[:, None], bounds


def attend(pieces, starts, seen, bounds):
    length = seen.shape[0]
    wide = pieces[0].shape[1]
    parts = QUERY_TILE // QUERY_PART
    return pl.pallas_call(
        attention_kernel,
        out_shape=jax.ShapeDtypeStruct((length, HEAD_DIM), jnp.bfloat16),
        grid_spec=pltpu.PrefetchScalarGridSpec(
            num_scalar_prefetch=2,
            grid=(length // QUERY_TILE,),
            in_specs=[pl.BlockSpec(memory_space=pl.ANY)] * 16
            + [pl.BlockSpec((QUERY_TILE, 1), lambda i, b, s: (i, 0))],
            out_specs=pl.BlockSpec((QUERY_TILE, HEAD_DIM), lambda i, b, s: (i, 0)),
            scratch_shapes=[
                pltpu.VMEM((length, wide), jnp.bfloat16),
                pltpu.VMEM((length, 2 * HEAD_DIM), jnp.bfloat16),
                pltpu.VMEM((parts, QUERY_PART, 1), jnp.float32),
                pltpu.VMEM((parts, QUERY_PART, 2 * HEAD_DIM), jnp.float32),
                pltpu.SemaphoreType.DMA((16, 4)),
            ],
        ),
        name="attend",
    )(bounds, starts, *pieces, seen)


def project_kernel(place, *refs):
    own, right, far_scored, far_latent, left, context, w_mine, w_other = refs[:8]
    outs, rows = refs[8:16], refs[16]
    step = pl.program_id(0)
    chunk = own.shape[1]

    @pl.when(step == 0)
    def _():
        found = [(own[0], own[1]), (right[0], right[1])]
        found += [(far_scored[...], far_latent[...]), (left[0], left[1])]
        for i, pair in enumerate(found):
            at = pl.ds(pl.multiple_of(place[4 + i] * chunk, chunk), chunk)
            for j in range(2):
                rows[j, at, :] = pair[j]

    role = place[step]
    source = rows[(role == 0).astype(jnp.int32)].astype(jnp.float32)
    source = source + context[...] * (role % 2).astype(jnp.float32)
    scale = lax.rsqrt(jnp.mean(source * source, axis=1, keepdims=True) + EPSILON)
    source = source.astype(jnp.bfloat16)
    columns = [
        w_mine[0, :, : 2 * HEAD_DIM],
        jnp.concatenate([w_mine[0, :, 2 * HEAD_DIM :], w_other[0, :, :HEAD_DIM]], axis=1),
        w_other[0, :, HEAD_DIM:],
    ]
    made = [
        jnp.dot(source, weights, preferred_element_type=jnp.float32) * scale for weights in columns
    ]
    queries = [made[0][:, :HEAD_DIM], made[1][:, HEAD_DIM:]]
    others = [[made[0][:, HEAD_DIM:], made[1][:, :HEAD_DIM]], [made[2]]]
    for i in range(4):

        @pl.when(step == i)
        def _():
            for side in range(2):
                out = outs[2 * i + side]
                out[:, :HEAD_DIM] = (queries[side] * SCORE_SCALE).astype(jnp.bfloat16)
                at = HEAD_DIM
                for part in others[side]:
                    out[:, at : at + part.shape[1]] = part.astype(jnp.bfloat16)
                    at += part.shape[1]


def project(place, rows, context, w_mine, w_other):
    chunk, width = rows[0].shape[1:]
    many = 4 * chunk
    columns = w_mine.shape[2]
    picked = pl.BlockSpec((1, width, columns), lambda t, r: ((r[t] + 1) // 2, 0, 0))
    whole = pl.BlockSpec(memory_space=pltpu.VMEM)
    return pl.pallas_call(
        project_kernel,
        out_shape=[jax.ShapeDtypeStruct((many, columns), jnp.bfloat16)] * 8,
        grid_spec=pltpu.PrefetchScalarGridSpec(
            num_scalar_prefetch=1,
            grid=(4,),
            in_specs=[whole] * 6 + [picked, picked],
            out_specs=[pl.BlockSpec((many, columns), lambda t, r: (0, 0))] * 8,
            scratch_shapes=[pltpu.VMEM((2, many, width), jnp.bfloat16)],
        ),
        name="project",
    )(place, *rows, context, w_mine, w_other)


def finish_kernel(place, *refs):
    attn, pending, latent, context = refs[:4]
    weights, block, terms = refs[4:20], refs[20], refs[21:]
    step = pl.program_id(0)
    branch = None
    for i in range(0, 16, 2):
        left = jnp.concatenate([attn[place[i]], attn[place[i + 1]]], axis=1)
        right = jnp.concatenate([weights[i][...], weights[i + 1][...]], axis=0)
        part = jnp.dot(left, right, preferred_element_type=jnp.float32)
        branch = part if branch is None else branch + part
    role = place[20]
    scored = pending[...].astype(jnp.float32) + context[...] * (role % 2).astype(jnp.float32)
    source = jnp.where(role == 0, latent[...].astype(jnp.float32), scored)
    block[...] = (source + branch).astype(jnp.bfloat16)
    weight = jnp.where(role == 2, GUIDE - 1.0, jnp.where(role == 3, 1.0, 0.0))
    weight = jnp.where(role == 1, -GUIDE, weight)
    for i, term in enumerate(terms):

        @pl.when(step == i)
        def _():
            term[...] = (weight * branch).astype(jnp.bfloat16)


def finish(place, attn, pending, latent, context, weights):
    rows, width = pending.shape
    inner = weights[0].shape[0]
    part = width // 4
    columns = pl.BlockSpec((rows, part), lambda t, s: (0, s[16 + t]))
    return pl.pallas_call(
        finish_kernel,
        out_shape=[jax.ShapeDtypeStruct((rows, width), jnp.bfloat16)]
        + [jax.ShapeDtypeStruct((rows, part), jnp.bfloat16)] * 4,
        grid_spec=pltpu.PrefetchScalarGridSpec(
            num_scalar_prefetch=1,
            grid=(4,),
            in_specs=[
                pl.BlockSpec(memory_space=pltpu.VMEM),
                columns,
                columns,
                pl.BlockSpec((1, part), lambda t, s: (0, s[16 + t])),
            ]
            + [pl.BlockSpec((inner, part), lambda t, s: (0, s[16 + t]))] * 16,
            out_specs=[columns] + [pl.BlockSpec((rows, part), lambda t, s: (0, 0))] * 4,
        ),
        name="finish",
    )(place, attn, pending, latent, context, *weights)


def place_kernel(starts, *refs):
    out = refs[-1]
    for i, piece in enumerate(refs[:-1]):
        rows, columns = piece.shape
        row = pl.multiple_of(starts[i, 0], rows)
        column = pl.multiple_of(starts[i, 1], columns)
        out[pl.ds(row, rows), pl.ds(column, columns)] = piece[...].astype(jnp.float32)


def place_all(starts, pieces, shape):
    vmem = pl.BlockSpec(memory_space=pltpu.VMEM)
    return pl.pallas_call(
        place_kernel,
        out_shape=jax.ShapeDtypeStruct(shape, jnp.float32),
        in_specs=[pl.BlockSpec(memory_space=pltpu.SMEM)] + [vmem] * len(pieces),
        out_specs=vmem,
        name="place_all",
    )(starts, *pieces)


def moved(axis, size, step):
    return [(i, (i + step) % size) for i in range(size)]


def moved(axis, size, step):
    return [(i, (i + step) % size) for i in range(size)]


def per_device(roles, block_ids, latent, pending, context, w_qkv, w_out, stored_attn):
    section, core = lax.axis_index("section"), lax.axis_index("core")
    section_role = lax.dynamic_index_in_dim(roles, section, 0, keepdims=False)
    is_generator = section_role == 0
    rows, _ = latent.shape[1:]
    chunk = rows // lax.axis_size("section")

    quarter = jnp.stack(
        [
            lax.dynamic_slice_in_dim(pending[0], section * chunk, chunk, 0),
            lax.dynamic_slice_in_dim(latent[0], section * chunk, chunk, 0),
        ]
    )
    w_proj = lax.dynamic_index_in_dim(w_out, (section_role + 1) // 2, 0, keepdims=False)
    inner = w_proj.shape[0]
    w_there = lax.ppermute(w_proj, "zhi", SWAP)
    w_swapped = [lax.ppermute(w_proj, "core", SWAP)]
    frame_ids = jnp.where(is_generator, block_ids[0, 0], block_ids[1, 0])
    seen, bounds = visibility(frame_ids)

    w_other = lax.ppermute(w_qkv, "core", SWAP)
    roles_here = jnp.roll(roles, -section)
    zhi = lax.axis_index("zhi")
    ahead = (lax.axis_index("x") + jnp.arange(4, dtype=jnp.int32)) % 4
    place = jnp.concatenate([roles_here, ahead])
    theirs = lax.ppermute(quarter, "zhi", SWAP)
    pieces, arrived = [], []
    for i, ours in enumerate((quarter, theirs)):
        left = lax.ppermute(ours, "x", moved("x", 4, 1))
        right = lax.ppermute(ours, "x", moved("x", 4, -1))
        far_scored = lax.ppermute(left[0], "x", moved("x", 4, 1))
        far_latent = lax.ppermute(right[1], "x", moved("x", 4, -1))
        gathered = [ours, right, far_scored, far_latent, left]
        if i:
            gathered, w_here, w_there = lax.optimization_barrier((gathered, w_proj, w_there))
        made = project(place, gathered, context, w_qkv, w_other)
        for step in (2, 1, 3, 0):
            for side in range(2):
                piece = made[2 * step + side]
                if step or side:
                    perm = [
                        (s * 2 + c, (s + step) % 4 * 2 + (c + side) % 2)
                        for s in range(4)
                        for c in range(2)
                    ]
                    piece = lax.ppermute(piece, ("section", "core"), perm)
                pieces.append(piece)
                arrived.append((i, step, side))
    w_swapped.append(lax.ppermute(w_there, "core", SWAP))
    left = [lax.ppermute(v, "x", moved("x", 4, 1)) for v in (w_here, w_there)]
    right = [lax.ppermute(v, "x", moved("x", 4, -1)) for v in (w_here, w_there)]
    far = [
        lax.ppermute(left[0], "x", moved("x", 4, 1)),
        lax.ppermute(right[1], "x", moved("x", 4, -1)),
    ]
    near = right + left
    w_swapped += [lax.ppermute(v, "core", SWAP) for v in near]
    half, step, side = jnp.array(arrived, jnp.int32).T
    starts = (zhi + half) % 2 * 8 + (core + side) % 2 * 4 + (section - step) % 4
    attn = attend(pieces, starts, seen, bounds)
    attn = lax.all_to_all(attn.reshape(16, rows, inner), SEQ, 0, 0, tiled=True)
    w_swapped += [lax.ppermute(v, "core", SWAP) for v in far]
    w_held = [w_here, w_there] + near + far
    chips = [(0, 0), (0, 1), (1, 0), (1, 1), (3, 0), (3, 1), (2, 0), (2, 1)]
    weights, heads = [], []
    for i, (dx, dz) in enumerate(chips):
        chip = (lax.axis_index("x") + dx) % 4 * 2 + (zhi + dz) % 2
        weights += [w_held[i], w_swapped[i]]
        heads += [chip * 2 + core, chip * 2 + 1 - core]
    targets = [(section + step) % 4 for step in (2, 1, 3, 0)]
    block, *terms = finish(
        jnp.stack(heads + targets + [section_role]), attn, pending[0], latent[0], context, weights
    )
    attn, stored_attn = lax.optimization_barrier((attn, stored_attn))
    stored = lax.all_to_all(stored_attn.reshape(8, 2 * rows, inner), RING, 0, 0, tiled=True)
    return (block[None, None],) + gradients(terms, stored)


def gradients(terms, stored):
    rows, part = terms[0].shape
    width = 4 * part
    sections = lax.axis_size("section")
    section, core = lax.axis_index("section"), lax.axis_index("core")
    total = None
    for step, term in zip((2, 1, 3, 0), terms):
        if step:
            term = lax.ppermute(term, "section", moved("section", sections, step))
        total = term.astype(jnp.float32) + (0.0 if total is None else total)
    grad_bf = total.astype(jnp.bfloat16)
    other = lax.ppermute(grad_bf, "core", SWAP)
    both = jnp.where(core == 0, jnp.stack([grad_bf, other]), jnp.stack([other, grad_bf]))
    both = both.reshape(2 * rows, part)
    inner = stored.shape[2]
    product = jnp.einsum("hri,rc->hic", stored, both, preferred_element_type=jnp.float32)
    product = product.astype(jnp.bfloat16).reshape(16, inner // 2, part)
    product = lax.all_to_all(product, RING + ("dp",), 0, 0, tiled=True)
    summed = jnp.sum(product.astype(jnp.float32), axis=0).astype(jnp.bfloat16)
    summed = jnp.broadcast_to(summed[None], (8,) + summed.shape)
    summed = lax.all_to_all(summed, ("section", "dp"), 0, 0, tiled=True)
    grad_out = summed.reshape(4, 2, inner // 2, part).transpose(1, 2, 0, 3)
    grad_out = grad_out.reshape(inner, width).astype(jnp.float32)
    groups, starts = [grad_bf], [section * part]
    for step in (2, 1, 3):
        groups.append(lax.ppermute(grad_bf, "section", moved("section", sections, step)))
        starts.append((section - step) % sections * part)
    gradient = place_all(
        jnp.stack([jnp.stack([jnp.zeros_like(s), s]) for s in starts]), groups, (rows, width)
    )
    return (gradient[None], grad_out)


def solution(mesh):
    fine = Mesh(mesh.devices.reshape(4, 4, 2, 2, 2), ("section", "x", "zhi", "core", "dp"))
    placed = (
        P(),
        P(None, "dp", None),
        P("dp", SEQ, None),
        P("dp", SEQ, None),
        P("dp", None),
        P(None, None, SEQ),
        P(None, SEQ, None),
        P("dp", None, SEQ),
    )
    return jax.shard_map(
        per_device,
        mesh=fine,
        in_specs=placed,
        out_specs=(P("section", "dp", SEQ, None), P("dp", SEQ, None), P(SEQ, None)),
        check_vma=False,
    )
```

```python
import jax
import jax.numpy as jnp
from jax import lax
from jax.experimental import pallas as pl
from jax.experimental.pallas import tpu as pltpu
from jax.sharding import Mesh
from jax.sharding import PartitionSpec as P


HEAD_DIM = 128
GUIDE = 3.0
EPSILON = 1e-06
NEGATIVE = -1e30
QUERY_TILE = 1024
QUERY_PART = 256
KEY_TILE = 1536
SCORE_SCALE = 1.4426950408889634 * HEAD_DIM ** (-0.5)
RING = ("x", "zhi")
SEQ = ("x", "zhi", "core")
SWAP = [(0, 1), (1, 0)]


def attention_kernel(bounds, starts, *refs):
    pieces = refs[:2]
    seen, out, qkv, values, top, acc, sems = refs[2:]
    tile = pl.program_id(0)
    length = qkv.shape[0]
    ring = 4
    chunk = pieces[0].shape[1] // ring

    @pl.when(tile == 0)
    def _():
        copies = []
        for i in range(16):
            half, section, core = i // 8, i % 8 // 2, i % 2
            for b in range(ring):
                place = (starts[half] + core * 4 + section) * chunk + b * (length // ring)
                place = pl.multiple_of(place, chunk)
                copies.append(
                    pltpu.make_async_copy(
                        pieces[half].at[i % 8, pl.ds(b * chunk, chunk)],
                        qkv.at[pl.ds(place, chunk)],
                        sems.at[i, b],
                    )
                )
        for copy in copies:
            copy.start()
        for copy in copies:
            copy.wait()
        values[:, :HEAD_DIM] = qkv[:, 2 * HEAD_DIM :]
        values[:, HEAD_DIM:] = jnp.ones((length, HEAD_DIM), jnp.bfloat16)

    top[...] = jnp.full(top.shape, NEGATIVE, jnp.float32)
    acc[...] = jnp.zeros(acc.shape, jnp.float32)
    parts = QUERY_TILE // QUERY_PART

    def step(j, masked):
        first = pl.multiple_of(j * KEY_TILE, KEY_TILE)
        keys = qkv[pl.ds(first, KEY_TILE), HEAD_DIM : 2 * HEAD_DIM]
        value = values[pl.ds(first, KEY_TILE), :]
        scores = []
        for i in range(parts):
            start = pl.multiple_of(tile * QUERY_TILE + i * QUERY_PART, QUERY_PART)
            score = lax.dot_general(
                qkv[pl.ds(start, QUERY_PART), :HEAD_DIM],
                keys,
                (((1,), (1,)), ((), ())),
                preferred_element_type=jnp.float32,
            )
            if masked:
                place = lax.broadcasted_iota(jnp.int32, score.shape, 1) + first
                limit = seen[pl.ds(i * QUERY_PART, QUERY_PART), :]
                score = jnp.where(place < limit, score, NEGATIVE)
            scores.append(score)
        olds = [top[i] for i in range(parts)]
        news = [
            jnp.maximum(old, jnp.max(score, axis=1, keepdims=True))
            for old, score in zip(olds, scores)
        ]
        for i in range(parts):
            weights = jnp.exp2(scores[i] - news[i]).astype(jnp.bfloat16)
            acc[i] = acc[i] * jnp.exp2(olds[i] - news[i]) + jnp.dot(
                weights, value, preferred_element_type=jnp.float32
            )
            top[i] = news[i]

    whole = bounds[tile, 0]

    @pl.loop(0, whole)
    def _(j):
        step(j, False)

    @pl.loop(whole, bounds[tile, 1])
    def _(j):
        step(j, True)

    for i in range(parts):
        out[pl.ds(i * QUERY_PART, QUERY_PART), :] = (
            acc[i, :, :HEAD_DIM] / acc[i, :, HEAD_DIM:]
        ).astype(jnp.bfloat16)


def visibility(frame_ids):
    length = frame_ids.shape[0]
    tiles = length // QUERY_TILE
    seen = jnp.sum((frame_ids[None, :] <= frame_ids[:, None]).astype(jnp.int32), axis=1)
    per_tile = seen.reshape(tiles, QUERY_TILE)
    bounds = jnp.stack(
        [per_tile[:, 0] // KEY_TILE, (per_tile[:, -1] + KEY_TILE - 1) // KEY_TILE], axis=1
    )
    return seen[:, None], bounds


def attend(pieces, starts, seen, bounds):
    length = seen.shape[0]
    wide = pieces[0].shape[2]
    parts = QUERY_TILE // QUERY_PART
    return pl.pallas_call(
        attention_kernel,
        out_shape=jax.ShapeDtypeStruct((length, HEAD_DIM), jnp.bfloat16),
        grid_spec=pltpu.PrefetchScalarGridSpec(
            num_scalar_prefetch=2,
            grid=(length // QUERY_TILE,),
            in_specs=[pl.BlockSpec(memory_space=pl.ANY)] * 2
            + [pl.BlockSpec((QUERY_TILE, 1), lambda i, b, s: (i, 0))],
            out_specs=pl.BlockSpec((QUERY_TILE, HEAD_DIM), lambda i, b, s: (i, 0)),
            scratch_shapes=[
                pltpu.VMEM((length, wide), jnp.bfloat16),
                pltpu.VMEM((length, 2 * HEAD_DIM), jnp.bfloat16),
                pltpu.VMEM((parts, QUERY_PART, 1), jnp.float32),
                pltpu.VMEM((parts, QUERY_PART, 2 * HEAD_DIM), jnp.float32),
                pltpu.SemaphoreType.DMA((16, 4)),
            ],
        ),
        name="attend",
    )(bounds, starts, *pieces, seen)


def project_kernel(place, *refs):
    own, right, far_scored, far_latent, left, context, w_mine, w_other = refs[:8]
    out, rows = refs[8:]
    step = pl.program_id(0)
    chunk = own.shape[1]

    @pl.when(step == 0)
    def _():
        found = [(own[0], own[1]), (right[0], right[1])]
        found += [(far_scored[...], far_latent[...]), (left[0], left[1])]
        for i, pair in enumerate(found):
            at = pl.ds(pl.multiple_of(place[4 + i] * chunk, chunk), chunk)
            for j in range(2):
                rows[j, at, :] = pair[j]

    role = place[step]
    source = rows[(role == 0).astype(jnp.int32)].astype(jnp.float32)
    source = source + context[...] * (role % 2).astype(jnp.float32)
    scale = lax.rsqrt(jnp.mean(source * source, axis=1, keepdims=True) + EPSILON)
    source = source.astype(jnp.bfloat16)
    columns = [
        w_mine[0, :, : 2 * HEAD_DIM],
        jnp.concatenate([w_mine[0, :, 2 * HEAD_DIM :], w_other[0, :, :HEAD_DIM]], axis=1),
        w_other[0, :, HEAD_DIM:],
    ]
    made = [
        jnp.dot(source, weights, preferred_element_type=jnp.float32) * scale for weights in columns
    ]
    queries = [made[0][:, :HEAD_DIM], made[1][:, HEAD_DIM:]]
    others = [[made[0][:, HEAD_DIM:], made[1][:, :HEAD_DIM]], [made[2]]]
    for side in range(2):
        slot = step * 2 + (place[8] + side) % 2
        out[slot, :, :HEAD_DIM] = (queries[side] * SCORE_SCALE).astype(jnp.bfloat16)
        at = HEAD_DIM
        for part in others[side]:
            out[slot, :, at : at + part.shape[1]] = part.astype(jnp.bfloat16)
            at += part.shape[1]


def project(place, rows, context, w_mine, w_other):
    chunk, width = rows[0].shape[1:]
    many = 4 * chunk
    columns = w_mine.shape[2]
    picked = pl.BlockSpec((1, width, columns), lambda t, r: ((r[t] + 1) // 2, 0, 0))
    whole = pl.BlockSpec(memory_space=pltpu.VMEM)
    return pl.pallas_call(
        project_kernel,
        out_shape=jax.ShapeDtypeStruct((8, many, columns), jnp.bfloat16),
        grid_spec=pltpu.PrefetchScalarGridSpec(
            num_scalar_prefetch=1,
            grid=(4,),
            in_specs=[whole] * 6 + [picked, picked],
            out_specs=pl.BlockSpec((8, many, columns), lambda t, r: (0, 0, 0)),
            scratch_shapes=[pltpu.VMEM((2, many, width), jnp.bfloat16)],
        ),
        name="project",
    )(place, *rows, context, w_mine, w_other)


def finish_kernel(place, *refs):
    attn, pending, latent, context = refs[:4]
    weights, (block, *terms) = refs[4:20], refs[-3:]
    step = pl.program_id(0)
    branch = None
    for i in range(0, 16, 2):
        left = jnp.concatenate([attn[place[i]], attn[place[i + 1]]], axis=1)
        right = jnp.concatenate([weights[i][...], weights[i + 1][...]], axis=0)
        part = jnp.dot(left, right, preferred_element_type=jnp.float32)
        branch = part if branch is None else branch + part
    role = place[20]
    scored = pending[...].astype(jnp.float32) + context[...] * (role % 2).astype(jnp.float32)
    source = jnp.where(role == 0, latent[...].astype(jnp.float32), scored)
    block[...] = (source + branch).astype(jnp.bfloat16)
    weight = jnp.where(role == 2, GUIDE - 1.0, jnp.where(role == 3, 1.0, 0.0))
    weight = jnp.where(role == 1, -GUIDE, weight)
    for i, term in enumerate(terms):

        @pl.when(step == i)
        def _():
            term[...] = (weight * branch).astype(jnp.bfloat16)


def finish(place, attn, pending, latent, context, weights, block=None):
    rows, width = pending.shape
    inner = weights[0].shape[0]
    part = width // 4
    earlier = [] if block is None else [block]
    skip = 16 + 2 * len(earlier)
    columns = pl.BlockSpec((rows, part), lambda t, s: (0, s[skip + t]))
    return pl.pallas_call(
        finish_kernel,
        out_shape=[jax.ShapeDtypeStruct((rows, width), jnp.bfloat16)]
        + [jax.ShapeDtypeStruct((rows, part), jnp.bfloat16)] * 2,
        grid_spec=pltpu.PrefetchScalarGridSpec(
            num_scalar_prefetch=1,
            grid=(2,),
            in_specs=[
                pl.BlockSpec(memory_space=pltpu.VMEM),
                columns,
                columns,
                pl.BlockSpec((1, part), lambda t, s: (0, s[skip + t])),
            ]
            + [pl.BlockSpec((inner, part), lambda t, s: (0, s[skip + t]))] * 16
            + [pl.BlockSpec(memory_space=pl.ANY)] * len(earlier),
            out_specs=[columns] + [pl.BlockSpec((rows, part), lambda t, s: (0, 0))] * 2,
        ),
        input_output_aliases={21: 0} if earlier else {},
        name="finish",
    )(place, attn, pending, latent, context, *weights, *earlier)


def place_kernel(starts, *refs):
    out = refs[-1]
    for i, piece in enumerate(refs[:-1]):
        rows, columns = piece.shape
        row = pl.multiple_of(starts[i, 0], rows)
        column = pl.multiple_of(starts[i, 1], columns)
        out[pl.ds(row, rows), pl.ds(column, columns)] = piece[...].astype(jnp.float32)


def place_all(starts, pieces, shape):
    vmem = pl.BlockSpec(memory_space=pltpu.VMEM)
    return pl.pallas_call(
        place_kernel,
        out_shape=jax.ShapeDtypeStruct(shape, jnp.float32),
        in_specs=[pl.BlockSpec(memory_space=pltpu.SMEM)] + [vmem] * len(pieces),
        out_specs=vmem,
        name="place_all",
    )(starts, *pieces)


def product_kernel(owners, *refs):
    stored, (own, other, out, both) = refs[:8], refs[8:]
    rows = own.shape[0]
    core = owners[8]
    both[pl.ds(pl.multiple_of(core * rows, rows), rows), :] = own[...]
    both[pl.ds(pl.multiple_of((1 - core) * rows, rows), rows), :] = other[...]
    for i, piece in enumerate(stored):
        out[owners[i]] = lax.dot_general(
            piece[...], both[...], (((0,), (0,)), ((), ())), preferred_element_type=jnp.float32
        ).astype(jnp.bfloat16)


def total_kernel(parts, out):
    total = jnp.sum(parts[...].astype(jnp.float32), axis=0).astype(jnp.bfloat16)
    for i in range(out.shape[0]):
        out[i] = total


def layout_kernel(parts, out):
    rows, columns = parts.shape[1:]
    for i in range(parts.shape[0]):
        at = i % 2 * rows, i // 2 * columns
        out[at[0] : at[0] + rows, at[1] : at[1] + columns] = parts[i].astype(jnp.float32)


def moved(axis, size, step):
    return [(i, (i + step) % size) for i in range(size)]


def moved(axis, size, step):
    return [(i, (i + step) % size) for i in range(size)]


def per_device(roles, block_ids, latent, pending, context, w_qkv, w_out, stored_attn):
    section, core = lax.axis_index("section"), lax.axis_index("core")
    section_role = lax.dynamic_index_in_dim(roles, section, 0, keepdims=False)
    is_generator = section_role == 0
    rows, _ = latent.shape[1:]
    chunk = rows // lax.axis_size("section")

    quarter = jnp.stack(
        [
            lax.dynamic_slice_in_dim(pending[0], section * chunk, chunk, 0),
            lax.dynamic_slice_in_dim(latent[0], section * chunk, chunk, 0),
        ]
    )
    w_proj = lax.dynamic_index_in_dim(w_out, (section_role + 1) // 2, 0, keepdims=False)
    inner = w_proj.shape[0]
    w_there = lax.ppermute(w_proj, "zhi", SWAP)
    w_swapped = [lax.ppermute(w_proj, "core", SWAP)]
    frame_ids = jnp.where(is_generator, block_ids[0, 0], block_ids[1, 0])
    seen, bounds = visibility(frame_ids)

    w_other = lax.ppermute(w_qkv, "core", SWAP)
    zhi = lax.axis_index("zhi")
    ahead = (lax.axis_index("x") + jnp.arange(4, dtype=jnp.int32)) % 4
    place = jnp.concatenate([roles, ahead, core[None]])
    theirs = lax.ppermute(quarter, "zhi", SWAP)
    pieces = []
    for i, ours in enumerate((quarter, theirs)):
        where = ("own", "other")[i]
        left = lax.ppermute(ours, "x", moved("x", 4, 1))
        right = lax.ppermute(ours, "x", moved("x", 4, -1))
        far_scored = lax.ppermute(left[0], "x", moved("x", 4, 1))
        far_latent = lax.ppermute(right[1], "x", moved("x", 4, -1))
        gathered = [ours, right, far_scored, far_latent, left]
        if i:
            gathered, w_here, w_there = lax.optimization_barrier((gathered, w_proj, w_there))
        made = project(place, gathered, context, w_qkv, w_other)
        pieces.append(lax.all_to_all(made, ("section", "core"), 0, 0, tiled=True))
    starts = (zhi + jnp.arange(2, dtype=jnp.int32)) % 2 * 8
    w_swapped.append(lax.ppermute(w_there, "core", SWAP))
    left = [lax.ppermute(v, "x", moved("x", 4, 1)) for v in (w_here, w_there)]
    right = [lax.ppermute(v, "x", moved("x", 4, -1)) for v in (w_here, w_there)]
    far = [
        lax.ppermute(left[0], "x", moved("x", 4, 1)),
        lax.ppermute(right[1], "x", moved("x", 4, -1)),
    ]
    near = right + left
    w_swapped += [lax.ppermute(v, "core", SWAP) for v in near]
    heads = []
    for dx, dz in ((0, 0), (0, 1), (1, 0), (1, 1), (3, 0), (3, 1), (2, 0), (2, 1)):
        chip = (lax.axis_index("x") + dx) % 4 * 2 + (zhi + dz) % 2
        heads += [chip * 2 + core, chip * 2 + 1 - core]
    where = jnp.stack(
        heads + [(section + step) % 4 for step in (2, 1, 3, 0)] + [section_role]
    )
    stored, owners = [], []
    for dx, dz in ((0, 0), (0, 1), (1, 0), (1, 1), (3, 0), (3, 1), (2, 0), (2, 1)):
        chip = (lax.axis_index("x") + dx) % 4 * 2 + (zhi + dz) % 2
        piece = lax.dynamic_slice_in_dim(stored_attn[0], chip * 2 * rows, 2 * rows, 0)
        if dx or dz:
            perm = [
                (i * 2 + j, (i + dx) % 4 * 2 + (j + dz) % 2) for i in range(4) for j in range(2)
            ]
            piece = lax.ppermute(piece, RING, perm)
        stored.append(piece)
        owners.append((lax.axis_index("x") - dx) % 4 * 2 + (zhi + dz) % 2)
    owners = jnp.stack(owners + [core])
    attn = attend(pieces, starts, seen, bounds)
    attn = lax.all_to_all(attn.reshape(16, rows, inner), SEQ, 0, 0, tiled=True)
    w_swapped += [lax.ppermute(v, "core", SWAP) for v in far]
    w_held = [w_here, w_there] + near + far
    weights = [v for pair in zip(w_held, w_swapped) for v in pair]
    block, terms = None, []
    for _ in range(2):
        block, *made = finish(where, attn, pending[0], latent[0], context, weights, block)
        terms += made
    return (block[None, None],) + gradients(terms, stored, owners)


def gradients(terms, stored, owners):
    rows, part = terms[0].shape
    width = 4 * part
    sections = lax.axis_size("section")
    section = lax.axis_index("section")
    total = None
    for step, term in zip((2, 1, 3, 0), terms):
        if step:
            term = lax.ppermute(term, "section", moved("section", sections, step))
        total = term.astype(jnp.float32) + (0.0 if total is None else total)
    grad_bf = total.astype(jnp.bfloat16)
    other = lax.ppermute(grad_bf, "core", SWAP)
    inner = stored[0].shape[1]
    vmem = pl.BlockSpec(memory_space=pltpu.VMEM)
    product = pl.pallas_call(
        product_kernel,
        out_shape=jax.ShapeDtypeStruct((8, inner, part), jnp.bfloat16),
        in_specs=[pl.BlockSpec(memory_space=pltpu.SMEM)] + [vmem] * 10,
        out_specs=vmem,
        scratch_shapes=[pltpu.VMEM((2 * rows, part), jnp.bfloat16)],
        name="product",
    )(owners, *stored, grad_bf, other)
    product = product.reshape(16, inner // 2, part)
    product = lax.all_to_all(product, RING + ("dp",), 0, 0, tiled=True)
    summed = pl.pallas_call(
        total_kernel,
        out_shape=jax.ShapeDtypeStruct((8,) + product.shape[1:], jnp.bfloat16),
        name="total",
    )(product)
    summed = lax.all_to_all(summed, ("section", "dp"), 0, 0, tiled=True)
    grad_out = pl.pallas_call(
        layout_kernel,
        out_shape=jax.ShapeDtypeStruct((inner, width), jnp.float32),
        name="layout",
    )(summed)
    groups, starts = [grad_bf], [section * part]
    for step in (2, 1, 3):
        groups.append(lax.ppermute(grad_bf, "section", moved("section", sections, step)))
        starts.append((section - step) % sections * part)
    gradient = place_all(
        jnp.stack([jnp.stack([jnp.zeros_like(s), s]) for s in starts]), groups, (rows, width)
    )
    return (gradient[None], grad_out)


def solution(mesh):
    fine = Mesh(mesh.devices.reshape(4, 4, 2, 2, 2), ("section", "x", "zhi", "core", "dp"))
    placed = (
        P(),
        P(None, "dp", None),
        P("dp", SEQ, None),
        P("dp", SEQ, None),
        P("dp", None),
        P(None, None, SEQ),
        P(None, SEQ, None),
        P("dp", None, SEQ),
    )
    return jax.shard_map(
        per_device,
        mesh=fine,
        in_specs=placed,
        out_specs=(P("section", "dp", SEQ, None), P("dp", SEQ, None), P(SEQ, None)),
        check_vma=False,
    )
```
